1024 devices in a mesh: dp: 16 (over z), expert: 64 (over x, y, core).
Axes of the slice: x: 4, y: 8, z: 16, core: 2. Of those that a mesh axis runs over, the one named last changes fastest.
Arguments:
- tokens: bfloat16 [4096, 7168], P('expert', 'dp'), may hold values from -6 to 6
- route_ids: int32 [4096, 8], P('expert'), may hold values from 0 to 255, as said below
- route_weight: bfloat16 [4096, 8], P('expert'), may hold values from 0.099609375 to 1
- out_cot: bfloat16 [4096, 7168], P('expert', 'dp'), may hold values from -6 to 6
- base_codes: bfloat16 [64, 2, 7168, 1024], P('expert', None, 'dp'), may hold values from -4 to 4
- base_scales: float32 [64, 2, 8, 7168], P('expert', None, None, 'dp'), may hold values from 0.004 to 0.03
- adapter_down: bfloat16 [64, 2, 32, 7168], P('expert', None, None, 'dp'), may hold values from -0.25 to 0.25
- adapter_up: bfloat16 [64, 2, 32, 1024], P('expert'), may hold values from -0.29882812 to 0.29882812
- magnitude: float32 [64, 2, 1024], P('expert'), may hold values from 0.5 to 2
- down_codes: bfloat16 [64, 1024, 7168], P('expert', None, 'dp'), may hold values from -4 to 4
- down_scales: float32 [64, 8, 7168], P('expert', None, 'dp'), may hold values from 0.01 to 0.06
Outputs:
- layer_out: bfloat16 [4096, 7168], P('expert', 'dp')
- input_grad: bfloat16 [4096, 7168], P('expert', 'dp')
- grad_adapter_down: float32 [64, 2, 32, 7168], P('expert', None, None, 'dp')
- grad_adapter_up: float32 [64, 2, 32, 1024], P('expert')
- grad_magnitude: float32 [64, 2, 1024], P('expert')
The draws below stay inside these ranges and needn't reach their ends.
Inputs may be any that keep to these rules, and one draw needn't show every extreme that they name: `route_ids`: each row names 8 different experts. In each aligned block of 64 rows no expert is named by more than 3 rows, and one expert below 64 is named by exactly 3 rows in every block.
All inputs are finite; a program needn't handle non-finite values.
Results may differ from the reference program's by a relative error of at most 0.03.
Values may be sent and summed in bfloat16 or wider, within the bound.
A program may use at most 32 MiB of HBM per device.

```python
import math
import jax
import jax.numpy as jnp
from jax import lax

D = 7168
EXPERTS_ALL = 256
TOPK = 8
FF = 1024
R = 32
QBLK = 128
TOK_DEV = 64
FFB = 8
EXPERTS = 64
CAP = 3
TOKENS = 4096
N_DP = 16
N_EXPERT = 64


def draw_route_ids(key, part):
    mean_load = TOK_DEV * TOPK // EXPERTS_ALL
    extra = CAP - mean_load
    hottest = jax.random.randint(jax.random.fold_in(key, 7), (), 0, EXPERTS)

    def one_block(block_index):
        block_key = jax.random.fold_in(key, block_index + 11)
        shuffled = jax.random.permutation(jax.random.fold_in(block_key, 1), EXPERTS_ALL)
        hot_place = jnp.argmax(shuffled == hottest)
        leading = shuffled[0]
        shuffled = shuffled.at[hot_place].set(leading).at[0].set(hottest)
        spread_vals = jax.random.randint(jax.random.fold_in(block_key, 2), (EXPERTS_ALL // 2,), 0, extra + 1)
        spread_vals = spread_vals.at[0].set(extra)
        counts = jnp.stack([mean_load + spread_vals, mean_load - spread_vals], axis=1).reshape(EXPERTS_ALL)
        boundary = jnp.cumsum(counts)
        places = jnp.arange(TOK_DEV * TOPK, dtype=jnp.int32)
        chosen = jnp.searchsorted(boundary, places, side='right')
        id_table = shuffled[chosen].reshape(TOPK, TOK_DEV).T
        row_order = jax.random.permutation(jax.random.fold_in(block_key, 3), TOK_DEV)
        return id_table[row_order]
    blocks = jax.vmap(one_block)(jnp.arange(N_EXPERT, dtype=jnp.int32))
    return blocks.reshape(N_EXPERT * TOK_DEV, TOPK).astype(jnp.int32)


def shared_direction(key):
    return jax.random.normal(jax.random.fold_in(key, 101), (EXPERTS, 2, D), jnp.float32)


def draw_adapter_down(key, part):
    direction = shared_direction(key)
    random_part = jax.random.normal(jax.random.fold_in(key, 102), (EXPERTS, 2, R, D), jnp.float32)
    strength = jax.random.uniform(jax.random.fold_in(key, 103), (EXPERTS, 2, R), jnp.float32, 0.6, 1.2)
    row_sign = (2 * jax.random.randint(jax.random.fold_in(key, 104), (EXPERTS, 2, R), 0, 2) - 1).astype(jnp.float32)
    levels = jnp.exp(jax.random.uniform(jax.random.fold_in(key, 105), (EXPERTS, 2, N_DP), jnp.float32, -1.5, 1.0))
    level_full = jnp.repeat(levels, D // N_DP, axis=2)
    row_values = (strength * row_sign)[:, :, :, None] * direction[:, :, None, :] + random_part
    return jnp.clip(0.02 * level_full[:, :, None, :] * row_values, -0.25, 0.25).astype(jnp.bfloat16)


def draw_base_codes(key, part):
    direction = shared_direction(key)
    random_part = jax.random.normal(jax.random.fold_in(key, 106), (EXPERTS, 2, D, FF), jnp.float32)
    column = jax.random.normal(jax.random.fold_in(key, 107), (EXPERTS, 2, FF), jnp.float32)
    code_values = 0.835 * random_part + 0.55 * direction[:, :, :, None] * column[:, :, None, :]
    return jnp.clip(code_values, -4.0, 4.0).astype(jnp.bfloat16)


def block_levels(key, shape, pieces, low, top_value):
    factor_of = 1.0
    for dim, parts in pieces:
        draws = jax.random.uniform(jax.random.fold_in(jax.random.fold_in(key, 6), dim), (parts,), jnp.float32, low / len(pieces), top_value / len(pieces))
        factor_of = factor_of * jnp.repeat(jnp.exp(draws), shape[dim] // parts).reshape((-1,) + (1,) * (len(shape) - 1 - dim))
    return factor_of


def centred(stream_key, shape, scale, most, split=(), kind=jnp.bfloat16):
    loudness = block_levels(stream_key, shape, split, -0.22, 0.18) if split else 1.0
    array = jax.random.normal(stream_key, shape, jnp.float32) * scale * loudness
    return jnp.minimum(jnp.maximum(array, -most), most).astype(kind)


def setup_inputs(seed: int = 0) -> dict:
    seeds = jax.random.split(jax.random.key(seed), 12)
    tokens = centred(seeds[0], (TOKENS, D), 1.0, 6.0, ((0, 64), (1, 16)))
    route_ids = draw_route_ids(jax.random.fold_in(seeds[11], 71), 0)
    route_weight = jnp.clip(0.099609375 + 0.9003906 * jax.random.uniform(seeds[2], (TOKENS, TOPK), jnp.float32) ** block_levels(seeds[2], (TOKENS, TOPK), ((0, 64),), -0.2, 0.2), 0.099609375, 1.0).astype(jnp.bfloat16)
    out_cot = centred(seeds[3], (TOKENS, D), 1.0, 6.0, ((0, 64), (1, 16)))
    base_codes = draw_base_codes(jax.random.fold_in(seeds[11], 71), 0)
    base_scales = jnp.clip(jnp.exp(math.log(0.03) - 2.014903 * jax.random.uniform(seeds[5], (EXPERTS, 2, FFB, D), jnp.float32) ** block_levels(seeds[5], (EXPERTS, 2, FFB, D), ((0, 64), (3, 16)), -0.2, 0.2)), 0.004, 0.03)
    adapter_down = draw_adapter_down(jax.random.fold_in(seeds[11], 71), 0)
    adapter_up = centred(seeds[7], (EXPERTS, 2, R, FF), 0.05, 0.29882812, ((0, 64),))
    magnitude = jnp.clip(jnp.exp(math.log(2.0) - 1.3862944 * jax.random.uniform(seeds[8], (EXPERTS, 2, FF), jnp.float32) ** block_levels(seeds[8], (EXPERTS, 2, FF), ((0, 64),), -0.2, 0.2)), 0.5, 2.0)
    down_codes = centred(seeds[9], (EXPERTS, FF, D), 1.0, 4.0, ((0, 64), (2, 16)))
    down_scales = jnp.clip(jnp.exp(math.log(0.06) - 1.7917595 * jax.random.uniform(seeds[10], (EXPERTS, FFB, D), jnp.float32) ** block_levels(seeds[10], (EXPERTS, FFB, D), ((0, 64), (2, 16)), -0.2, 0.2)), 0.01, 0.06)
    return {"tokens": tokens, "route_ids": route_ids, "route_weight": route_weight, "out_cot": out_cot, "base_codes": base_codes, "base_scales": base_scales, "adapter_down": adapter_down, "adapter_up": adapter_up, "magnitude": magnitude, "down_codes": down_codes, "down_scales": down_scales}


EPSILON = 1e-06
HIGHEST = lax.Precision.HIGHEST

def reference(tokens, route_ids, route_weight, out_cot, base_codes, base_scales, adapter_down, adapter_up, magnitude, down_codes, down_scales):
    local_width = D // N_DP
    slot_total = N_EXPERT * CAP
    blocks = route_ids.reshape(N_EXPERT, TOK_DEV, TOPK)
    weights = route_weight.reshape(N_EXPERT, TOK_DEV, TOPK).astype(jnp.float32)
    expert_ids = jnp.arange(EXPERTS, dtype=jnp.int32)
    matches = blocks[:, :, :, None] == expert_ids
    present = lax.optimization_barrier(jnp.sum(matches.astype(jnp.int32), axis=2))
    weight_of = lax.optimization_barrier(jnp.sum(jnp.where(matches, weights[:, :, :, None], 0.0), axis=2))
    position = jnp.cumsum(present, axis=1) - present
    slot_ids = jnp.arange(CAP, dtype=jnp.int32)
    token_ids = jnp.arange(TOK_DEV, dtype=jnp.int32)
    block_start = (jnp.arange(N_EXPERT, dtype=jnp.int32) * TOK_DEV)[:, None]

    def per_expert(carry, expert_index):
        out_sum, grad_sum = carry
        present_e = present[:, :, expert_index]
        position_e = position[:, :, expert_index]
        weight_e = weight_of[:, :, expert_index]
        choose = (present_e[:, None, :] == 1) & (position_e[:, None, :] == slot_ids[None, :, None])
        filled = jnp.any(choose, axis=2).reshape(slot_total)[:, None]
        slot_token = lax.optimization_barrier(jnp.sum(jnp.where(choose, token_ids[None, None, :], 0), axis=2)).astype(jnp.int32)
        slot_weight = lax.optimization_barrier(jnp.sum(jnp.where(choose, weight_e[:, None, :], 0.0), axis=2)).reshape(slot_total)[:, None]
        rows_global = (block_start + slot_token).reshape(slot_total).astype(jnp.int32)
        expert_in = jnp.where(filled, tokens[rows_global], jnp.zeros((), jnp.bfloat16))
        route_cot = jnp.where(filled, slot_weight * out_cot[rows_global].astype(jnp.float32), 0.0).astype(jnp.bfloat16)
        scale_full = jnp.repeat(jnp.swapaxes(base_scales[expert_index], 1, 2), QBLK, axis=2)
        dequant = base_codes[expert_index].astype(jnp.float32) * scale_full
        down_f = adapter_down[expert_index].astype(jnp.float32)
        up_f = adapter_up[expert_index].astype(jnp.float32)
        adapted = dequant + jnp.einsum('ird,irf->idf', down_f, up_f, precision=HIGHEST)
        adapted_b = adapted.astype(jnp.bfloat16)
        col_norm = jnp.sqrt(lax.optimization_barrier(jnp.sum(adapted * adapted, axis=1)) + EPSILON)
        mag = magnitude[expert_index]
        mag_ratio = mag / col_norm
        in_blocks = expert_in.astype(jnp.float32).reshape(slot_total, N_DP, local_width)
        weight_blocks = adapted_b.astype(jnp.float32).reshape(2, N_DP, local_width, FF)
        partial_value = jnp.einsum('spd,ipdf->psif', in_blocks, weight_blocks, precision=HIGHEST)
        pre_act = lax.optimization_barrier(jnp.sum(lax.optimization_barrier(partial_value.astype(jnp.bfloat16)).astype(jnp.float32), axis=0))
        gate_val = pre_act[:, 0] * mag_ratio[0]
        up_val = pre_act[:, 1] * mag_ratio[1]
        sigmoid_val = jax.nn.sigmoid(gate_val)
        silu_val = gate_val * sigmoid_val
        hidden = (silu_val * up_val).astype(jnp.bfloat16)
        down_scale = jnp.repeat(down_scales[expert_index], QBLK, axis=0)
        down_base = (down_codes[expert_index].astype(jnp.float32) * down_scale).astype(jnp.bfloat16)
        expert_out = jnp.dot(hidden, down_base, preferred_element_type=jnp.float32).astype(jnp.bfloat16)
        cot_blocks = route_cot.astype(jnp.float32).reshape(slot_total, N_DP, local_width)
        down_blocks = down_base.astype(jnp.float32).reshape(FF, N_DP, local_width)
        unit_part = jnp.einsum('spd,fpd->psf', cot_blocks, down_blocks, precision=HIGHEST)
        unit_grad = lax.optimization_barrier(jnp.sum(lax.optimization_barrier(unit_part.astype(jnp.bfloat16)).astype(jnp.float32), axis=0))
        gate_grad = unit_grad * up_val * sigmoid_val * (1.0 + gate_val * (1.0 - sigmoid_val))
        up_grad = unit_grad * silu_val
        pre_grad = jnp.stack([gate_grad, up_grad], axis=1)
        mag_grad = lax.optimization_barrier(jnp.sum(pre_grad * pre_act, axis=0)) / col_norm
        scaled = (pre_grad * mag_ratio[None]).astype(jnp.bfloat16)
        shrink = mag * mag_grad / (col_norm * col_norm)
        scaled_f = scaled.astype(jnp.float32)
        slot_grad = jnp.einsum('sif,idf->sd', scaled_f, adapted_b.astype(jnp.float32), precision=HIGHEST).astype(jnp.bfloat16)
        low_in = jnp.einsum('sd,ird->sir', expert_in.astype(jnp.float32), down_f, precision=HIGHEST).astype(jnp.bfloat16)
        rank_proj = jnp.einsum('ird,idf->irf', down_f, adapted, precision=HIGHEST)
        rank_back = jnp.einsum('sif,irf->sir', scaled_f, up_f, precision=HIGHEST).astype(jnp.bfloat16)
        grad_down = jnp.einsum('sir,sd->ird', rank_back.astype(jnp.float32), expert_in.astype(jnp.float32), precision=HIGHEST)
        grad_down = grad_down - jnp.einsum('irf,idf->ird', up_f * shrink[:, None, :], adapted, precision=HIGHEST)
        grad_up = jnp.einsum('sir,sif->irf', low_in.astype(jnp.float32), scaled_f, precision=HIGHEST)
        grad_up = grad_up - rank_proj * shrink[:, None, :]
        out_sum = out_sum.at[rows_global].add(jnp.where(filled, slot_weight * expert_out.astype(jnp.float32), 0.0))
        grad_sum = grad_sum.at[rows_global].add(jnp.where(filled, slot_grad.astype(jnp.float32), 0.0))
        return ((out_sum, grad_sum), (grad_down, grad_up, mag_grad))
    zeros = jnp.zeros((TOKENS, D), jnp.float32)
    carried, stacked = lax.scan(per_expert, (zeros, zeros), jnp.arange(EXPERTS, dtype=jnp.int32))
    out_sum, grad_sum = carried
    grad_down, grad_up, mag_grad = stacked
    return (out_sum.astype(jnp.bfloat16), grad_sum.astype(jnp.bfloat16), grad_down, grad_up, mag_grad)
```

```python
import jax
import jax.numpy as jnp
from jax import lax
from jax.experimental import pallas as pl
from jax.experimental.pallas import tpu as pltpu
from jax.sharding import PartitionSpec as P

EPSILON = 1e-06
MESH = pl.DeviceIdType.MESH
F32 = jnp.float32
BF16 = jnp.bfloat16
NZ = 16
NE = 64
RS_ROWS = 304
AG_ROWS = 352
RS_SUBS = ((0, 96), (96, 96), (192, 112))
AG_SUBS = ((0, 112), (112, 112), (224, 128))
NSUB = 3


def nn(a, b):
    return jnp.dot(a, b, preferred_element_type=F32)


def nt(a, b):
    return lax.dot_general(a, b, (((1,), (1,)), ((), ())), preferred_element_type=F32)


def iota(shape, dim):
    return lax.broadcasted_iota(jnp.int32, shape, dim)


def split(v):
    hi = v.astype(BF16)
    return hi, (v - hi.astype(F32)).astype(BF16)


def kernel(
    tok_ref,
    ids_ref,
    w_ref,
    cot_ref,
    codes_hbm,
    scales_ref,
    down_ref,
    up_ref,
    mag_ref,
    dcodes_hbm,
    dscales_ref,
    layer_ref,
    igrad_ref,
    gdown_ref,
    gup_ref,
    gmag_ref,
    codes,
    dcodes,
    hi,
    lo,
    dbase,
    xin,
    tpose,
    upad,
    perm,
    gt_ref,
    colsq,
    dpad,
    send1,
    recv1,
    send2,
    recv2,
    xs,
    cs,
    yback,
    eown,
    erecv,
    own,
    rbuf,
    lbuf,
    ag,
    hid,
    sgu,
    lowt,
    rank,
    wsem,
    s1s,
    s1r,
    s2s,
    s2r,
    es,
    er,
    rrs,
    rrr,
    rls,
    rlr,
    ars,
    arr,
    als,
    alr,
):
    me = lax.axis_index("expert")
    z = lax.axis_index("dp")
    mx = lax.div(me, 16)
    my = lax.rem(lax.div(me, 2), 8)
    mc = lax.rem(me, 2)
    right = lax.rem(z + 1, NZ)
    left = lax.rem(z + NZ - 1, NZ)

    def peer_of(k):
        px = lax.rem(mx + lax.div(k, 16), 4)
        py = lax.rem(my + lax.rem(lax.div(k, 2), 8), 8)
        pc = lax.rem(mc + lax.rem(k, 2), 2)
        return (px * 8 + py) * 2 + pc

    wcopy = pltpu.make_async_copy(codes_hbm, codes, wsem.at[0])
    dcopy = pltpu.make_async_copy(dcodes_hbm, dcodes, wsem.at[1])
    wcopy.start()
    dcopy.start()

    barrier = pltpu.get_barrier_semaphore()

    @pl.loop(1, NE)
    def _(k):
        pl.semaphore_signal(
            barrier, inc=1, device_id={"expert": peer_of(k)}, device_id_type=MESH
        )

    @pl.loop(1, NZ)
    def _(k):
        pl.semaphore_signal(
            barrier, inc=1, device_id={"dp": lax.rem(z + k, NZ)}, device_id_type=MESH
        )

    ids2 = jnp.concatenate([ids_ref[...], ids_ref[...]], axis=0)
    w2 = jnp.concatenate([w_ref[...], w_ref[...]], axis=0).astype(F32)
    shape = (128, 512)
    col = iota(shape, 1)
    exp_of = lax.shift_right_logical(col, 3)
    present = jnp.zeros(shape, F32)
    wt = jnp.zeros(shape, F32)
    for k in range(8):
        match = ids2[:, k : k + 1] == exp_of
        present = present + jnp.where(match, 1.0, 0.0)
        wt = wt + jnp.where(match, w2[:, k : k + 1], 0.0)
    ti = iota((128, 128), 0)
    tj = iota((128, 128), 1)
    tri = jnp.where((tj < ti) & ((tj >= 64) == (ti >= 64)), 1.0, 0.0).astype(BF16)
    position = nn(tri, present.astype(BF16))
    lane_c = (col & 3).astype(F32)
    choose = jnp.where((present > 0.5) & (position == lane_c), 1.0, 0.0)
    chosen_w = choose * wt
    row_low = iota(shape, 0) < 64
    j_low = (col & 7) < 4
    dt = jnp.where(row_low, jnp.where(j_low, choose, 0.0), jnp.where(j_low, 0.0, chosen_w))
    gt = jnp.where(row_low, jnp.where(j_low, chosen_w, 0.0), jnp.where(j_low, 0.0, choose))
    gt_ref[...] = gt.astype(BF16)

    xin[:, 384:512] = jnp.zeros((128, 128), BF16)
    xin[0:64, 0:448] = tok_ref[...]
    xin[64:128, 0:448] = cot_ref[...]
    disp = nn(dt.T.astype(BF16), xin[...])
    s0 = disp[:, 0:256].reshape(NE, 8, 256)
    s1 = disp[:, 256:512].reshape(NE, 8, 256)
    send1[...] = jnp.concatenate([s0, s1], axis=1).reshape(NE * 16, 256).astype(BF16).reshape(NE, 16, 256)

    pl.semaphore_wait(barrier, NE - 1 + NZ - 1)

    def exchange(src, dst, ssem, rsem):
        def copy(k, slot, peer):
            return pltpu.make_async_remote_copy(
                src_ref=src.at[peer],
                dst_ref=dst.at[slot],
                send_sem=ssem.at[k],
                recv_sem=rsem.at[slot],
                device_id={"expert": peer},
                device_id_type=MESH,
            )

        @pl.loop(1, NE)
        def _(k):
            copy(k, me, peer_of(k)).start()

        dst[me] = src[me]

        def wait():
            @pl.loop(1, NE)
            def _(k):
                peer = peer_of(k)
                copy(k, peer, peer).wait_recv()

        def drain():
            @pl.loop(1, NE)
            def _(k):
                copy(k, me, peer_of(k)).wait_send()

        return wait, drain

    wait1, drain1 = exchange(send1, recv1, s1s, s1r)

    tpose[80:128, :] = jnp.zeros((48, 512), F32)
    tpose[0:80, 384:512] = jnp.zeros((80, 128), F32)
    tpose[0:16, 0:448] = scales_ref[...]
    tpose[16:80, 0:448] = down_ref[...].astype(F32)
    dpad[:, 384:512] = jnp.zeros((64, 128), BF16)
    dpad[:, 0:448] = down_ref[...]
    turned = tpose[...].T
    for i in range(4):
        tpose[:, i * 128 : (i + 1) * 128] = turned[i * 128 : (i + 1) * 128, :]
    upad[...] = jnp.zeros((2, 128, 1024), BF16)
    upad[0, 16:48, :] = up_ref[0]
    upad[1, 48:80, :] = up_ref[1]
    hi[:, 448:512, :] = jnp.zeros((2, 64, 1024), BF16)
    lo[:, 448:512, :] = jnp.zeros((2, 64, 1024), BF16)
    colsq[...] = jnp.zeros((16, 1024), F32)
    wcopy.wait()

    for blk in range(7):
        d0 = blk * 64
        lane0 = (d0 // 128) * 128
        row0 = d0 % 128
        turn = tpose[row0 : row0 + 64, lane0 : lane0 + 128]
        turn_b = turn.astype(BF16)
        for i in range(2):
            for fb in range(8):
                f0 = fb * 128
                scale = turn[:, i * 8 + fb : i * 8 + fb + 1]
                val = codes[i, d0 : d0 + 64, f0 : f0 + 128].astype(F32) * scale
                val = val + nn(turn_b, upad[i, :, f0 : f0 + 128])
                top, bottom = split(val)
                hi[i, d0 : d0 + 64, f0 : f0 + 128] = top
                lo[i, d0 : d0 + 64, f0 : f0 + 128] = bottom
                sq = (val * val).reshape(8, 8, 128).sum(axis=0)
                colsq[i * 8 : i * 8 + 8, f0 : f0 + 128] = colsq[i * 8 : i * 8 + 8, f0 : f0 + 128] + sq

    for q in range(8):
        f0 = q * 128
        c0 = jnp.sum(colsq[0:8, f0 : f0 + 128], axis=0, keepdims=True)
        c1 = jnp.sum(colsq[8:16, f0 : f0 + 128], axis=0, keepdims=True)
        rows = iota((16, 128), 0)
        cblock = jnp.where(rows == 0, c0, jnp.where(rows == 1, c1, 0.0)).astype(BF16)
        for h in range(2):
            dn = dpad[h * 32 : (h + 1) * 32, :]
            proj = nn(dn, hi[h, :, f0 : f0 + 128]) + nn(dn, lo[h, :, f0 : f0 + 128])
            eown[2 * q + h, 0:32, :] = proj.astype(BF16)
            eown[2 * q + h, 32:48, :] = cblock

    def early(k, slot, peer):
        return pltpu.make_async_remote_copy(
            src_ref=eown.at[peer],
            dst_ref=erecv.at[slot],
            send_sem=es.at[k],
            recv_sem=er.at[slot],
            device_id={"dp": peer},
            device_id_type=MESH,
        )

    @pl.loop(1, NZ)
    def _(k):
        early(k, z, lax.rem(z + k, NZ)).start()

    dcopy.wait()
    dbase[:, 384:512] = jnp.zeros((1024, 128), BF16)
    for fb in range(8):
        f0 = fb * 128
        dbase[f0 : f0 + 128, 0:448] = (
            dcodes[f0 : f0 + 128, :].astype(F32) * dscales_ref[fb : fb + 1, :]
        ).astype(BF16)

    pr = iota((512, 512), 0)
    pc = iota((512, 512), 1)

    def target(v):
        return (
            16 * (v & 31)
            + (lax.shift_right_logical(v, 5) & 3)
            + 8 * (lax.shift_right_logical(v, 7) & 1)
            + 4 * lax.shift_right_logical(v, 8)
        )

    perm[0] = jnp.where(pc == target(pr), 1.0, 0.0).astype(BF16)
    perm[1] = jnp.where(pr == target(pc), 1.0, 0.0).astype(BF16)
    for p in range(8, NZ):
        own[p, 288:304, :] = jnp.zeros((16, 128), BF16)

    wait1()
    for h in range(2):
        block = recv1[h * 32 : (h + 1) * 32].reshape(512, 256)
        got = nn(perm[0], block).astype(BF16)
        xs[h, :, 0:256] = got[0:128]
        xs[h, :, 256:512] = got[128:256]
        cs[h, :, 0:256] = got[256:384]
        cs[h, :, 256:512] = got[384:512]

    low = nt(dpad[...], xs[...].reshape(256, 512)).astype(BF16)
    for p in range(8):
        own[p, 288:304, :] = low[(p // 2) * 16 : (p // 2) * 16 + 16, (p % 2) * 128 : (p % 2) * 128 + 128]
    for q in range(8):
        f0 = q * 128
        for h in range(2):
            p = 2 * q + h
            own[p, 0:96, :] = nn(xs[h, 0:96, :], hi[0, :, f0 : f0 + 128]).astype(BF16)
            own[p, 96:192, :] = nn(xs[h, 0:96, :], hi[1, :, f0 : f0 + 128]).astype(BF16)
            own[p, 192:288, :] = nt(cs[h, 0:96, :], dbase[f0 : f0 + 128, :]).astype(BF16)

    def hop(src, dst, ssem, rsem, to):
        return pltpu.make_async_remote_copy(
            src_ref=src,
            dst_ref=dst,
            send_sem=ssem,
            recv_sem=rsem,
            device_id={"dp": to},
            device_id_type=MESH,
        )

    def rs_copy(t, sub, rightward, first):
        r0, n = RS_SUBS[sub]
        buf, ssem, rsem, to = (rbuf, rrs, rrr, right) if rightward else (lbuf, rls, rlr, left)
        chunk = lax.rem(z + 7 - t, NZ) if rightward else lax.rem(z + 8 + t, NZ)
        src = own.at[chunk, pl.ds(r0, n), :] if first else buf.at[t - 1, pl.ds(r0, n), :]
        return chunk, hop(
            src, buf.at[t, pl.ds(r0, n), :], ssem.at[t * NSUB + sub], rsem.at[t * NSUB + sub], to
        )

    for sub in range(NSUB):
        for rightward in (True, False):
            rs_copy(0, sub, rightward, True)[1].start()

    def rs_step(t, rightward, sub):
        r0, n = RS_SUBS[sub]
        buf = rbuf if rightward else lbuf
        rs_copy(t - 1, sub, rightward, True)[1].wait_recv()
        chunk, copy = rs_copy(t, sub, rightward, False)
        buf[t - 1, pl.ds(r0, n), :] = (
            buf[t - 1, pl.ds(r0, n), :].astype(F32) + own[chunk, pl.ds(r0, n), :].astype(F32)
        ).astype(BF16)
        copy.start()

    @pl.loop(1, 7)
    def _(t):
        for sub in range(NSUB):
            for rightward in (True, False):
                rs_step(t, rightward, sub)

    for sub in range(NSUB):
        rs_step(7, False, sub)

    @pl.loop(1, NZ)
    def _(k):
        peer = lax.rem(z + k, NZ)
        early(k, peer, peer).wait_recv()

    erecv[z] = eown[z]
    esum = erecv[0].astype(F32)
    for p in range(1, NZ):
        esum = esum + erecv[p].astype(F32)
    q_lane = pl.multiple_of(lax.div(z, 2) * 128, 128)
    mag = mag_ref[:, pl.ds(q_lane, 128)]
    norm = jnp.sqrt(esum[32:34, :] + EPSILON)
    ratio = mag / norm

    for sub in range(NSUB):
        rs_copy(6, sub, True, True)[1].wait_recv()
        rs_copy(7, sub, False, True)[1].wait_recv()
    total = own[z].astype(F32) + rbuf[6].astype(F32) + lbuf[7].astype(F32)
    gate_pre, up_pre, unit = total[0:96], total[96:192], total[192:288]
    gate_val = gate_pre * ratio[0:1]
    up_val = up_pre * ratio[1:2]
    sig = jax.nn.sigmoid(gate_val)
    silu = gate_val * sig
    gate_grad = unit * up_val * sig * (1.0 + gate_val * (1.0 - sig))
    up_grad = unit * silu
    gm0 = jnp.sum(gate_grad * gate_pre, axis=0, keepdims=True) / norm[0:1]
    gm1 = jnp.sum(up_grad * up_pre, axis=0, keepdims=True) / norm[1:2]
    sh0 = mag[0:1] * gm0 / (norm[0:1] * norm[0:1])
    sh1 = mag[1:2] * gm1 / (norm[1:2] * norm[1:2])
    rows = iota((16, 128), 0)
    extra = jnp.where(
        rows == 0, gm0, jnp.where(rows == 1, gm1, jnp.where(rows == 2, sh0, jnp.where(rows == 3, sh1, 0.0)))
    )
    ag[z, 0:96, :] = (silu * up_val).astype(BF16)
    ag[z, 96:192, :] = (gate_grad * ratio[0:1]).astype(BF16)
    ag[z, 192:288, :] = (up_grad * ratio[1:2]).astype(BF16)
    ag[z, 288:304, :] = total[288:304].astype(BF16)
    ag[z, 304:336, :] = esum[0:32, :].astype(BF16)
    ag[z, 336:352, :] = extra.astype(BF16)

    def ag_copy(t, sub, rightward):
        r0, n = AG_SUBS[sub]
        ssem, rsem, to = (ars, arr, right) if rightward else (als, alr, left)
        chunk = lax.rem(z + NZ - t, NZ) if rightward else lax.rem(z + t, NZ)
        ref = ag.at[chunk, pl.ds(r0, n), :]
        return hop(ref, ref, ssem.at[t * NSUB + sub], rsem.at[t * NSUB + sub], to)

    def ag_arrived(t, sub, rightward):
        r0, n = AG_SUBS[sub]
        ssem, rsem, to = (ars, arr, right) if rightward else (als, alr, left)
        chunk = lax.rem(z + NZ - 1 - t, NZ) if rightward else lax.rem(z + 1 + t, NZ)
        ref = ag.at[chunk, pl.ds(r0, n), :]
        hop(ref, ref, ssem.at[t * NSUB + sub], rsem.at[t * NSUB + sub], to).wait_recv()

    for sub in range(NSUB):
        for rightward in (True, False):
            ag_copy(0, sub, rightward).start()

    @pl.loop(1, 7)
    def _(t):
        for sub in range(NSUB):
            for rightward in (True, False):
                ag_arrived(t - 1, sub, rightward)
                ag_copy(t, sub, rightward).start()

    for sub in range(NSUB):
        ag_arrived(6, sub, True)
        ag_copy(7, sub, True).start()
    for sub in range(NSUB):
        ag_arrived(6, sub, False)
    for sub in range(NSUB):
        ag_arrived(7, sub, True)

    for q in range(8):
        f0 = q * 128
        for h in range(2):
            p = 2 * q + h
            hid[h * 96 : (h + 1) * 96, f0 : f0 + 128] = ag[p, 0:96, :]
            sgu[0, h * 96 : (h + 1) * 96, f0 : f0 + 128] = ag[p, 96:192, :]
            sgu[1, h * 96 : (h + 1) * 96, f0 : f0 + 128] = ag[p, 192:288, :]

    yback[...] = jnp.zeros((2, 512, 256), BF16)
    out = nn(hid[...], dbase[...]).astype(BF16)
    back = (nt(sgu[0], hi[0]) + nt(sgu[1], hi[1])).astype(BF16)
    for h in range(2):
        r = slice(h * 96, (h + 1) * 96)
        yback[h, 0:96, :] = out[r, 0:256]
        yback[h, 128:224, :] = out[r, 256:512]
        yback[h, 256:352, :] = back[r, 0:256]
        yback[h, 384:480, :] = back[r, 256:512]
        send2[h * 32 : (h + 1) * 32] = nn(perm[1], yback[h]).astype(BF16).reshape(32, 16, 256)

    wait2, drain2 = exchange(send2, recv2, s2s, s2r)

    for q in range(8):
        f0 = q * 128
        both = ag[2 * q, 336:352, :].astype(F32) + ag[2 * q + 1, 336:352, :].astype(F32)
        gmag_ref[:, f0 : f0 + 128] = both[0:2]
        rank[64:72, f0 : f0 + 128] = both[0:8]
        rank[0:32, f0 : f0 + 128] = ag[2 * q, 304:336, :].astype(F32)
        rank[32:64, f0 : f0 + 128] = ag[2 * q + 1, 304:336, :].astype(F32)
    for p in range(8):
        lowt[(p // 2) * 16 : (p // 2) * 16 + 16, (p % 2) * 128 : (p % 2) * 128 + 128] = ag[p, 288:304, :]
    for i in range(2):
        shrink = rank[66 + i : 67 + i, :]
        back_t = nt(up_ref[i], sgu[i]).astype(BF16)
        down_t = nn(back_t[:, 0:96], xs[0, 0:96, :]) + nn(back_t[:, 96:192], xs[1, 0:96, :])
        uh, ul = split(up_ref[i].astype(F32) * shrink)
        down_t = down_t - (nt(uh, hi[i]) + nt(uh, lo[i]) + nt(ul, hi[i]))
        gdown_ref[i] = down_t[:, 0:448]
        rows_i = slice(i * 32, (i + 1) * 32)
        grow = nn(lowt[rows_i, 0:96], sgu[i, 0:96, :]) + nn(lowt[rows_i, 128:224], sgu[i, 96:192, :])
        gup_ref[i] = grow - rank[rows_i, :] * shrink

    wait2()
    got = recv2[...].astype(F32)
    g0 = nn(gt_ref[...], got[:, 0:8, :].reshape(512, 256).astype(BF16))
    g1 = nn(gt_ref[...], got[:, 8:16, :].reshape(512, 256).astype(BF16))
    layer_ref[:, 0:256] = g0[0:64].astype(BF16)
    layer_ref[:, 256:448] = g1[0:64, 0:192].astype(BF16)
    igrad_ref[:, 0:256] = g0[64:128].astype(BF16)
    igrad_ref[:, 256:448] = g1[64:128, 0:192].astype(BF16)

    drain1()
    drain2()

    @pl.loop(1, NZ)
    def _(k):
        early(k, z, lax.rem(z + k, NZ)).wait_send()

    @pl.loop(0, 7)
    def _(t):
        for sub in range(NSUB):
            rs_copy(t, sub, True, True)[1].wait_send()
            rs_copy(t, sub, False, True)[1].wait_send()
            ag_copy(t, sub, True).wait_send()
            ag_copy(t, sub, False).wait_send()

    for sub in range(NSUB):
        rs_copy(7, sub, False, True)[1].wait_send()
        ag_copy(7, sub, True).wait_send()


def body(tokens, route_ids, route_weight, out_cot, base_codes, base_scales, adapter_down, adapter_up, magnitude, down_codes, down_scales):
    vmem = pl.BlockSpec(memory_space=pltpu.VMEM)
    hbm = pl.BlockSpec(memory_space=pl.ANY)
    dma = pltpu.SemaphoreType.DMA
    outs = pl.pallas_call(
        kernel,
        out_shape=(
            jax.ShapeDtypeStruct((64, 448), BF16),
            jax.ShapeDtypeStruct((64, 448), BF16),
            jax.ShapeDtypeStruct((2, 32, 448), F32),
            jax.ShapeDtypeStruct((2, 32, 1024), F32),
            jax.ShapeDtypeStruct((2, 1024), F32),
        ),
        in_specs=[vmem, vmem, vmem, vmem, hbm, vmem, vmem, vmem, vmem, hbm, vmem],
        out_specs=(vmem,) * 5,
        scratch_shapes=[
            pltpu.VMEM((2, 448, 1024), BF16),
            pltpu.VMEM((1024, 448), BF16),
            pltpu.VMEM((2, 512, 1024), BF16),
            pltpu.VMEM((2, 512, 1024), BF16),
            pltpu.VMEM((1024, 512), BF16),
            pltpu.VMEM((128, 512), BF16),
            pltpu.VMEM((128, 512), F32),
            pltpu.VMEM((2, 128, 1024), BF16),
            pltpu.VMEM((2, 512, 512), BF16),
            pltpu.VMEM((128, 512), BF16),
            pltpu.VMEM((16, 1024), F32),
            pltpu.VMEM((64, 512), BF16),
            pltpu.VMEM((NE, 16, 256), BF16),
            pltpu.VMEM((NE, 16, 256), BF16),
            pltpu.VMEM((NE, 16, 256), BF16),
            pltpu.VMEM((NE, 16, 256), BF16),
            pltpu.VMEM((2, 128, 512), BF16),
            pltpu.VMEM((2, 128, 512), BF16),
            pltpu.VMEM((2, 512, 256), BF16),
            pltpu.VMEM((NZ, 48, 128), BF16),
            pltpu.VMEM((NZ, 48, 128), BF16),
            pltpu.VMEM((NZ, RS_ROWS, 128), BF16),
            pltpu.VMEM((7, RS_ROWS, 128), BF16),
            pltpu.VMEM((8, RS_ROWS, 128), BF16),
            pltpu.VMEM((NZ, AG_ROWS, 128), BF16),
            pltpu.VMEM((192, 1024), BF16),
            pltpu.VMEM((2, 192, 1024), BF16),
            pltpu.VMEM((64, 256), BF16),
            pltpu.VMEM((72, 1024), F32),
            dma((2,)),
            dma((NE,)),
            dma((NE,)),
            dma((NE,)),
            dma((NE,)),
            dma((NZ,)),
            dma((NZ,)),
            dma((7 * NSUB,)),
            dma((7 * NSUB,)),
            dma((8 * NSUB,)),
            dma((8 * NSUB,)),
            dma((8 * NSUB,)),
            dma((8 * NSUB,)),
            dma((7 * NSUB,)),
            dma((7 * NSUB,)),
        ],
        compiler_params=pltpu.CompilerParams(
            collective_id=0, has_side_effects=True, vmem_limit_bytes=56 * 1024 * 1024
        ),
    )(
        tokens,
        route_ids,
        route_weight,
        out_cot,
        base_codes[0],
        base_scales.reshape(16, 448),
        adapter_down.reshape(64, 448),
        adapter_up[0],
        magnitude[0],
        down_codes[0],
        down_scales[0],
    )
    layer_out, input_grad, grad_down, grad_up, grad_mag = outs
    return (layer_out, input_grad, grad_down[None], grad_up[None], grad_mag[None])


def solution(mesh):
    in_specs = (
        P("expert", "dp"),
        P("expert", None),
        P("expert", None),
        P("expert", "dp"),
        P("expert", None, "dp", None),
        P("expert", None, None, "dp"),
        P("expert", None, None, "dp"),
        P("expert", None, None, None),
        P("expert", None, None),
        P("expert", None, "dp"),
        P("expert", None, "dp"),
    )
    out_specs = (
        P("expert", "dp"),
        P("expert", "dp"),
        P("expert", None, None, "dp"),
        P("expert", None, None, None),
        P("expert", None, None),
    )
    return jax.shard_map(body, mesh=mesh, in_specs=in_specs, out_specs=out_specs, check_vma=False)
```

```python
import jax
import jax.numpy as jnp
from jax import lax
from jax.experimental import pallas as pl
from jax.experimental.pallas import tpu as pltpu
from jax.sharding import PartitionSpec as P

EPSILON = 1e-06
MESH = pl.DeviceIdType.MESH
F32 = jnp.float32
BF16 = jnp.bfloat16
NZ = 16
NE = 64
A_SUBS = ((0, 48), (48, 48), (96, 48), (144, 64))
B_SUBS = ((0, 48), (48, 48))
H_SUBS = ((0, 48), (48, 48), (96, 48))
S_SUBS = ((0, 48), (48, 48), (96, 48), (144, 64))


def nn(a, b):
    return jnp.dot(a, b, preferred_element_type=F32)


def nt(a, b):
    return lax.dot_general(a, b, (((1,), (1,)), ((), ())), preferred_element_type=F32)


def iota(shape, dim):
    return lax.broadcasted_iota(jnp.int32, shape, dim)


def split(v):
    hi = v.astype(BF16)
    return hi, (v - hi.astype(F32)).astype(BF16)


def kernel(
    tok_ref,
    ids_ref,
    w_ref,
    cot_ref,
    codes_hbm,
    scales_ref,
    down_ref,
    up_ref,
    mag_ref,
    dcodes_hbm,
    dscales_ref,
    layer_ref,
    igrad_ref,
    gdown_ref,
    gup_ref,
    gmag_ref,
    codes,
    dcodes,
    hi,
    lo,
    dbase,
    xin,
    xcot,
    tpose,
    upad,
    perm,
    gtc,
    gtw,
    colsq,
    dpad,
    send_in,
    recv_in,
    send_cot,
    recv_cot,
    send_out,
    recv_out,
    send_grad,
    recv_grad,
    xs,
    cs,
    yout,
    ygrad,
    eown,
    erecv,
    a_own,
    a_right,
    a_left,
    b_own,
    b_right,
    b_left,
    a_sum,
    ag_h,
    ag_s,
    hid,
    sgu,
    lowt,
    rank,
    wsem,
    in_s,
    in_r,
    cot_s,
    cot_r,
    out_s,
    out_r,
    grad_s,
    grad_r,
    es,
    er,
    a_rs,
    a_rr,
    a_ls,
    a_lr,
    b_rs,
    b_rr,
    b_ls,
    b_lr,
    h_rs,
    h_rr,
    h_ls,
    h_lr,
    s_rs,
    s_rr,
    s_ls,
    s_lr,
):
    me = lax.axis_index("expert")
    z = lax.axis_index("dp")
    mx = lax.div(me, 16)
    my = lax.rem(lax.div(me, 2), 8)
    mc = lax.rem(me, 2)
    right = lax.rem(z + 1, NZ)
    left = lax.rem(z + NZ - 1, NZ)
    mate = me + 1 - 2 * mc

    wcopy = pltpu.make_async_copy(codes_hbm, codes, wsem.at[0])
    dcopy = pltpu.make_async_copy(dcodes_hbm, dcodes, wsem.at[1])
    wcopy.start()
    dcopy.start()

    def chip_of(o):
        px = lax.rem(mx + lax.div(o, 8), 4)
        py = lax.rem(my + lax.rem(o, 8), 8)
        return (px * 8 + py) * 2

    def for_peers(fn, lo_chip=0, hi_chip=32):
        if lo_chip == 0:
            fn(1, mate)

        @pl.loop(max(lo_chip, 1), hi_chip)
        def _(o):
            chip = chip_of(o)
            fn(2 * o, chip + mc)
            fn(2 * o + 1, chip + 1 - mc)

    barrier = pltpu.get_barrier_semaphore()
    for_peers(
        lambda k, peer: pl.semaphore_signal(
            barrier, inc=1, device_id={"expert": peer}, device_id_type=MESH
        )
    )

    @pl.loop(1, NZ)
    def _(k):
        pl.semaphore_signal(
            barrier, inc=1, device_id={"dp": lax.rem(z + k, NZ)}, device_id_type=MESH
        )

    dup = jnp.where((iota((64, 128), 1) & 63) == iota((64, 128), 0), 1.0, 0.0).astype(BF16)
    ids2 = nn(ids_ref[...].astype(F32).astype(BF16), dup)
    w2 = nn(w_ref[...], dup)
    shape = (512, 128)
    row = iota(shape, 0)
    col = iota(shape, 1)
    exp_of = lax.shift_right_logical(row, 3).astype(F32)
    present = jnp.zeros(shape, F32)
    wt = jnp.zeros(shape, F32)
    for k in range(8):
        match = ids2[k : k + 1, :] == exp_of
        present = present + jnp.where(match, 1.0, 0.0)
        wt = wt + jnp.where(match, w2[k : k + 1, :], 0.0)
    ti = iota((128, 128), 0)
    tj = iota((128, 128), 1)
    tri = jnp.where((ti < tj) & ((tj >= 64) == (ti >= 64)), 1.0, 0.0).astype(BF16)
    position = nn(present.astype(BF16), tri)
    slot = (row & 3).astype(F32)
    same_half = (lax.shift_right_logical(row, 2) & 1) == lax.shift_right_logical(col, 6)
    choose = jnp.where((present > 0.5) & (position == slot) & same_half, 1.0, 0.0)
    chosen_w = choose * wt

    def stack(dst, src):
        dst[64:128, 128:256] = jnp.zeros((64, 128), BF16)
        dst[0:64, :] = src[:, 0:256]
        dst[64:128, 0:192] = src[:, 256:448]

    stack(xin, tok_ref)
    stack(xcot, cot_ref)
    send_in[...] = nn(choose.astype(BF16), xin[...]).reshape(NE, 8, 256).astype(BF16)
    send_cot[...] = nn(chosen_w.astype(BF16), xcot[...]).reshape(NE, 8, 256).astype(BF16)

    pl.semaphore_wait(barrier, NE - 1 + NZ - 1)

    class Exchange:
        def __init__(self, src, dst, ssem, rsem):
            self.src, self.dst, self.ssem, self.rsem = src, dst, ssem, rsem

        def copy(self, k, slot, peer):
            return pltpu.make_async_remote_copy(
                src_ref=self.src.at[peer],
                dst_ref=self.dst.at[slot],
                send_sem=self.ssem.at[k],
                recv_sem=self.rsem.at[slot],
                device_id={"expert": peer},
                device_id_type=MESH,
            )

        def start(self, lo_chip=0, hi_chip=32):
            for_peers(lambda k, peer: self.copy(k, me, peer).start(), lo_chip, hi_chip)

        def keep(self):
            self.dst[me] = self.src[me]

        def wait(self):
            for_peers(lambda k, peer: self.copy(k, peer, peer).wait_recv())

        def drain(self):
            for_peers(lambda k, peer: self.copy(k, me, peer).wait_send())

    x_in = Exchange(send_in, recv_in, in_s, in_r)
    x_cot = Exchange(send_cot, recv_cot, cot_s, cot_r)
    x_out = Exchange(send_out, recv_out, out_s, out_r)
    x_grad = Exchange(send_grad, recv_grad, grad_s, grad_r)
    x_in.start()
    x_cot.start()
    x_in.keep()
    x_cot.keep()

    tpose[88:128, :] = jnp.zeros((40, 512), F32)
    tpose[0:88, 384:512] = jnp.zeros((88, 128), F32)
    tpose[0:16, 0:448] = scales_ref[...]
    tpose[16:80, 0:448] = down_ref[...].astype(F32)
    tpose[80:88, 0:448] = dscales_ref[...]
    dpad[:, 384:512] = jnp.zeros((64, 128), BF16)
    dpad[:, 0:448] = down_ref[...]
    turned = tpose[...].T
    for i in range(4):
        tpose[:, i * 128 : (i + 1) * 128] = turned[i * 128 : (i + 1) * 128, :]
    upad[...] = jnp.zeros((2, 128, 1024), BF16)
    upad[0, 16:48, :] = up_ref[0]
    upad[1, 48:80, :] = up_ref[1]
    hi[:, 448:512, :] = jnp.zeros((2, 64, 1024), BF16)
    lo[:, 448:512, :] = jnp.zeros((2, 64, 1024), BF16)
    dbase[448:512, :] = jnp.zeros((64, 1024), BF16)
    colsq[...] = jnp.zeros((16, 1024), F32)
    wcopy.wait()

    def turned_rows(blk):
        d0 = blk * 64
        return tpose[d0 % 128 : d0 % 128 + 64, (d0 // 128) * 128 : (d0 // 128) * 128 + 128]

    for blk in range(7):
        d0 = blk * 64
        turn = turned_rows(blk)
        turn_b = turn.astype(BF16)
        for i in range(2):
            for fb in range(8):
                f0 = fb * 128
                scale = turn[:, i * 8 + fb : i * 8 + fb + 1]
                val = codes[i, d0 : d0 + 64, f0 : f0 + 128].astype(F32) * scale
                val = val + nn(turn_b, upad[i, :, f0 : f0 + 128])
                top, bottom = split(val)
                hi[i, d0 : d0 + 64, f0 : f0 + 128] = top
                lo[i, d0 : d0 + 64, f0 : f0 + 128] = bottom
                sq = (val * val).reshape(8, 8, 128).sum(axis=0)
                colsq[i * 8 : i * 8 + 8, f0 : f0 + 128] = colsq[i * 8 : i * 8 + 8, f0 : f0 + 128] + sq

    for q in range(8):
        f0 = q * 128
        c0 = jnp.sum(colsq[0:8, f0 : f0 + 128], axis=0, keepdims=True)
        c1 = jnp.sum(colsq[8:16, f0 : f0 + 128], axis=0, keepdims=True)
        rows = iota((16, 128), 0)
        cblock = jnp.where(rows == 0, c0, jnp.where(rows == 1, c1, 0.0)).astype(BF16)
        for h in range(2):
            dn = dpad[h * 32 : (h + 1) * 32, :]
            proj = nn(dn, hi[h, :, f0 : f0 + 128]) + nn(dn, lo[h, :, f0 : f0 + 128])
            eown[2 * q + h, 0:32, :] = proj.astype(BF16)
            eown[2 * q + h, 32:48, :] = cblock

    def early(k, slot, peer):
        return pltpu.make_async_remote_copy(
            src_ref=eown.at[peer],
            dst_ref=erecv.at[slot],
            send_sem=es.at[k],
            recv_sem=er.at[slot],
            device_id={"dp": peer},
            device_id_type=MESH,
        )

    @pl.loop(1, NZ)
    def _(k):
        early(k, z, lax.rem(z + k, NZ)).start()

    pr = iota((256, 256), 0)
    pc = iota((256, 256), 1)

    def target(v):
        return (
            8 * (v & 31)
            + (lax.shift_right_logical(v, 5) & 3)
            + 4 * lax.shift_right_logical(v, 7)
        )

    perm[0] = jnp.where(pc == target(pr), 1.0, 0.0).astype(BF16)
    perm[1] = jnp.where(pr == target(pc), 1.0, 0.0).astype(BF16)
    for p in range(8, NZ):
        a_own[p, 192:208, :] = jnp.zeros((16, 128), BF16)
    yout[...] = jnp.zeros((2, 256, 256), BF16)
    ygrad[...] = jnp.zeros((2, 256, 256), BF16)

    dcopy.wait()
    for blk in range(7):
        d0 = blk * 64
        turn = turned_rows(blk)
        for fb in range(8):
            f0 = fb * 128
            dbase[d0 : d0 + 64, f0 : f0 + 128] = (
                dcodes[d0 : d0 + 64, f0 : f0 + 128].astype(F32) * turn[:, 80 + fb : 81 + fb]
            ).astype(BF16)
    gtc[...] = choose.T.astype(BF16)
    gtw[...] = chosen_w.T.astype(BF16)

    def arrange(recv, dst):
        for h in range(2):
            block = recv[h * 32 : (h + 1) * 32].astype(F32).reshape(256, 256).astype(BF16)
            got = nn(perm[0], block).astype(BF16)
            dst[h, :, 0:256] = got[0:128]
            dst[h, :, 256:512] = got[128:256]

    def lanes_of(c):
        return pl.ds(pl.multiple_of(lax.div(c, 2) * 128, 128), 128)

    def chunk_a(c):
        h = lax.rem(c, 2)
        rows = xs[h, 0:96, :]
        a_own[c, 0:96, :] = nn(rows, hi[0, :, lanes_of(c)]).astype(BF16)
        a_own[c, 96:192, :] = nn(rows, hi[1, :, lanes_of(c)]).astype(BF16)

    def chunk_b(c):
        h = lax.rem(c, 2)
        b_own[c] = nn(cs[h, 0:96, :], dbase[:, lanes_of(c)]).astype(BF16)

    def hop(src, dst, ssem, rsem, to):
        return pltpu.make_async_remote_copy(
            src_ref=src,
            dst_ref=dst,
            send_sem=ssem,
            recv_sem=rsem,
            device_id={"dp": to},
            device_id_type=MESH,
        )

    class Reduce:
        def __init__(self, own, bufs, sems, subs, make):
            self.own, self.bufs, self.sems, self.subs, self.make = own, bufs, sems, subs, make

        def chunk(self, t, d):
            return lax.rem(z + 7 - t, NZ) if d == 0 else lax.rem(z + 8 + t, NZ)

        def copy(self, t, sub, d, first):
            r0, n = self.subs[sub]
            buf, (ssem, rsem) = self.bufs[d], self.sems[d]
            rows = pl.ds(r0, n)
            src = self.own.at[self.chunk(t, d), rows, :] if first else buf.at[t - 1, rows, :]
            at = t * len(self.subs) + sub
            return hop(src, buf.at[t, rows, :], ssem.at[at], rsem.at[at], (right, left)[d])

        def begin(self):
            for d in (0, 1):
                self.make(self.chunk(0, d))
                for sub in range(len(self.subs)):
                    self.copy(0, sub, d, True).start()

        def step(self, t, dirs=(0, 1)):
            for d in dirs:
                self.make(self.chunk(t, d))
            for sub in range(len(self.subs)):
                r0, n = self.subs[sub]
                rows = pl.ds(r0, n)
                for d in dirs:
                    buf = self.bufs[d]
                    self.copy(t - 1, sub, d, True).wait_recv()
                    buf[t - 1, rows, :] = (
                        buf[t - 1, rows, :].astype(F32)
                        + self.own[self.chunk(t, d), rows, :].astype(F32)
                    ).astype(BF16)
                    self.copy(t, sub, d, False).start()

        def total(self):
            for sub in range(len(self.subs)):
                self.copy(6, sub, 0, True).wait_recv()
                self.copy(7, sub, 1, True).wait_recv()
            return (
                self.own[z].astype(F32) + self.bufs[0][6].astype(F32) + self.bufs[1][7].astype(F32)
            )

        def drain(self):
            @pl.loop(0, 7)
            def _(t):
                for sub in range(len(self.subs)):
                    self.copy(t, sub, 0, True).wait_send()
                    self.copy(t, sub, 1, True).wait_send()

            for sub in range(len(self.subs)):
                self.copy(7, sub, 1, True).wait_send()

    class Gather:
        def __init__(self, buf, sems, subs):
            self.buf, self.sems, self.subs = buf, sems, subs

        def copy(self, t, sub, d, chunk):
            r0, n = self.subs[sub]
            ssem, rsem = self.sems[d]
            ref = self.buf.at[chunk, pl.ds(r0, n), :]
            at = t * len(self.subs) + sub
            return hop(ref, ref, ssem.at[at], rsem.at[at], (right, left)[d])

        def sent(self, t, sub, d):
            return self.copy(t, sub, d, lax.rem(z + NZ - t, NZ) if d == 0 else lax.rem(z + t, NZ))

        def come(self, t, sub, d):
            return self.copy(
                t, sub, d, lax.rem(z + NZ - 1 - t, NZ) if d == 0 else lax.rem(z + 1 + t, NZ)
            )

        def begin(self):
            for sub in range(len(self.subs)):
                for d in (0, 1):
                    self.sent(0, sub, d).start()

        def step(self, t, dirs=(0, 1)):
            for sub in range(len(self.subs)):
                for d in dirs:
                    self.come(t - 1, sub, d).wait_recv()
                    self.sent(t, sub, d).start()

        def finish(self):
            for sub in range(len(self.subs)):
                self.come(6, sub, 1).wait_recv()
            for sub in range(len(self.subs)):
                self.come(7, sub, 0).wait_recv()

        def drain(self):
            @pl.loop(0, 7)
            def _(t):
                for sub in range(len(self.subs)):
                    self.sent(t, sub, 0).wait_send()
                    self.sent(t, sub, 1).wait_send()

            for sub in range(len(self.subs)):
                self.sent(7, sub, 0).wait_send()

    red_a = Reduce(a_own, (a_right, a_left), ((a_rs, a_rr), (a_ls, a_lr)), A_SUBS, chunk_a)
    red_b = Reduce(b_own, (b_right, b_left), ((b_rs, b_rr), (b_ls, b_lr)), B_SUBS, chunk_b)
    gat_h = Gather(ag_h, ((h_rs, h_rr), (h_ls, h_lr)), H_SUBS)
    gat_s = Gather(ag_s, ((s_rs, s_rr), (s_ls, s_lr)), S_SUBS)

    x_in.wait()
    arrange(recv_in, xs)
    low = nt(dpad[...], xs[...].reshape(256, 512)).astype(BF16)
    for p in range(8):
        a_own[p, 192:208, :] = low[
            (p // 2) * 16 : (p // 2) * 16 + 16, (p % 2) * 128 : (p % 2) * 128 + 128
        ]
    red_a.begin()

    @pl.loop(1, 4)
    def _(t):
        red_a.step(t)

    x_cot.wait()
    arrange(recv_cot, cs)
    red_b.begin()

    @pl.loop(4, 7)
    def _(t):
        red_a.step(t)
        red_b.step(t - 3)

    red_a.step(7, (1,))
    chunk_a(z)
    red_b.step(4)
    chunk_b(z)

    @pl.loop(1, NZ)
    def _(k):
        peer = lax.rem(z + k, NZ)
        early(k, peer, peer).wait_recv()

    erecv[z] = eown[z]
    esum = erecv[0].astype(F32)
    for p in range(1, NZ):
        esum = esum + erecv[p].astype(F32)
    mag = mag_ref[:, lanes_of(z)]
    norm = jnp.sqrt(esum[32:34, :] + EPSILON)
    ratio = mag / norm

    total = red_a.total()
    a_sum[...] = total
    gate_val = total[0:96] * ratio[0:1]
    up_val = total[96:192] * ratio[1:2]
    ag_h[z, 0:96, :] = (gate_val * jax.nn.sigmoid(gate_val) * up_val).astype(BF16)
    ag_h[z, 96:112, :] = total[192:208].astype(BF16)
    ag_h[z, 112:144, :] = esum[0:32, :].astype(BF16)
    gat_h.begin()

    @pl.loop(5, 7)
    def _(t):
        red_b.step(t)
        gat_h.step(t - 4)

    red_b.step(7, (1,))
    gat_h.step(3)

    unit = red_b.total()
    gate_pre, up_pre = a_sum[0:96, :], a_sum[96:192, :]
    gate_val = gate_pre * ratio[0:1]
    up_val = up_pre * ratio[1:2]
    sig = jax.nn.sigmoid(gate_val)
    gate_grad = unit * up_val * sig * (1.0 + gate_val * (1.0 - sig))
    up_grad = unit * (gate_val * sig)
    gm0 = jnp.sum(gate_grad * gate_pre, axis=0, keepdims=True) / norm[0:1]
    gm1 = jnp.sum(up_grad * up_pre, axis=0, keepdims=True) / norm[1:2]
    sh0 = mag[0:1] * gm0 / (norm[0:1] * norm[0:1])
    sh1 = mag[1:2] * gm1 / (norm[1:2] * norm[1:2])
    rows = iota((16, 128), 0)
    extra = jnp.where(
        rows == 0, gm0, jnp.where(rows == 1, gm1, jnp.where(rows == 2, sh0, jnp.where(rows == 3, sh1, 0.0)))
    )
    ag_s[z, 0:96, :] = (gate_grad * ratio[0:1]).astype(BF16)
    ag_s[z, 96:192, :] = (up_grad * ratio[1:2]).astype(BF16)
    ag_s[z, 192:208, :] = extra.astype(BF16)
    gat_s.begin()

    @pl.loop(4, 7)
    def _(t):
        gat_h.step(t)
        gat_s.step(t - 3)

    gat_h.step(7, (0,))
    gat_s.step(4)
    gat_h.finish()

    def give_back(value, y, send):
        for h in range(2):
            r = slice(h * 96, (h + 1) * 96)
            y[h, 0:96, :] = value[r, 0:256]
            y[h, 128:224, :] = value[r, 256:512]
            send[h * 32 : (h + 1) * 32] = nn(perm[1], y[h]).reshape(32, 8, 256).astype(BF16)

    for q in range(8):
        f0 = q * 128
        for h in range(2):
            hid[h * 96 : (h + 1) * 96, f0 : f0 + 128] = ag_h[2 * q + h, 0:96, :]
    give_back(nt(hid[...], dbase[...]).astype(BF16), yout, send_out)
    gat_s.step(5)
    x_out.start(0, 16)
    gat_s.step(6)
    x_out.start(16, 32)
    gat_s.step(7, (0,))
    x_out.keep()
    gat_s.finish()

    for q in range(8):
        f0 = q * 128
        for h in range(2):
            sgu[0, h * 96 : (h + 1) * 96, f0 : f0 + 128] = ag_s[2 * q + h, 0:96, :]
            sgu[1, h * 96 : (h + 1) * 96, f0 : f0 + 128] = ag_s[2 * q + h, 96:192, :]
    give_back((nt(sgu[0], hi[0]) + nt(sgu[1], hi[1])).astype(BF16), ygrad, send_grad)
    x_grad.start()
    x_grad.keep()

    for q in range(8):
        f0 = q * 128
        both = ag_s[2 * q, 192:208, :].astype(F32) + ag_s[2 * q + 1, 192:208, :].astype(F32)
        gmag_ref[:, f0 : f0 + 128] = both[0:2]
        rank[64:72, f0 : f0 + 128] = both[0:8]
        rank[0:32, f0 : f0 + 128] = ag_h[2 * q, 112:144, :].astype(F32)
        rank[32:64, f0 : f0 + 128] = ag_h[2 * q + 1, 112:144, :].astype(F32)
    for p in range(8):
        lowt[(p // 2) * 16 : (p // 2) * 16 + 16, (p % 2) * 128 : (p % 2) * 128 + 128] = ag_h[p, 96:112, :]
    for i in range(2):
        shrink = rank[66 + i : 67 + i, :]
        back_t = nt(up_ref[i], sgu[i]).astype(BF16)
        down_t = nn(back_t[:, 0:96], xs[0, 0:96, :]) + nn(back_t[:, 96:192], xs[1, 0:96, :])
        uh, ul = split(up_ref[i].astype(F32) * shrink)
        down_t = down_t - (nt(uh, hi[i]) + nt(uh, lo[i]) + nt(ul, hi[i]))
        gdown_ref[i] = down_t[:, 0:448]
        rows_i = slice(i * 32, (i + 1) * 32)
        grow = nn(lowt[rows_i, 0:96], sgu[i, 0:96, :]) + nn(lowt[rows_i, 128:224], sgu[i, 96:192, :])
        gup_ref[i] = grow - rank[rows_i, :] * shrink

    x_in.drain()
    x_cot.drain()
    red_a.drain()
    red_b.drain()
    gat_h.drain()
    gat_s.drain()

    @pl.loop(1, NZ)
    def _(k):
        early(k, z, lax.rem(z + k, NZ)).wait_send()

    def combine(exchange, mat, recv, out):
        exchange.wait()
        got = nn(mat[...], recv[...].astype(F32).reshape(512, 256).astype(BF16)).astype(BF16)
        out[:, 0:256] = got[0:64]
        out[:, 256:448] = got[64:128, 0:192]

    combine(x_out, gtw, recv_out, layer_ref)
    combine(x_grad, gtc, recv_grad, igrad_ref)
    x_out.drain()
    x_grad.drain()


def emit(*refs):
    for src, dst in zip(refs[:5], refs[5:]):
        dst[...] = src[...]


def body(tokens, route_ids, route_weight, out_cot, base_codes, base_scales, adapter_down, adapter_up, magnitude, down_codes, down_scales):
    vmem = pl.BlockSpec(memory_space=pltpu.VMEM)
    hbm = pl.BlockSpec(memory_space=pl.ANY)
    dma = pltpu.SemaphoreType.DMA
    block = pltpu.VMEM((NE, 8, 256), BF16)
    out_shape = (
        jax.ShapeDtypeStruct((64, 448), BF16),
        jax.ShapeDtypeStruct((64, 448), BF16),
        jax.ShapeDtypeStruct((2, 32, 448), F32),
        jax.ShapeDtypeStruct((2, 32, 1024), F32),
        jax.ShapeDtypeStruct((2, 1024), F32),
    )
    outs = pl.pallas_call(
        kernel,
        out_shape=out_shape,
        in_specs=[vmem, vmem, vmem, vmem, hbm, vmem, vmem, vmem, vmem, hbm, vmem],
        out_specs=(vmem,) * 5,
        scratch_shapes=[
            pltpu.VMEM((2, 448, 1024), BF16),
            pltpu.VMEM((448, 1024), BF16),
            pltpu.VMEM((2, 512, 1024), BF16),
            pltpu.VMEM((2, 512, 1024), BF16),
            pltpu.VMEM((512, 1024), BF16),
            pltpu.VMEM((128, 256), BF16),
            pltpu.VMEM((128, 256), BF16),
            pltpu.VMEM((128, 512), F32),
            pltpu.VMEM((2, 128, 1024), BF16),
            pltpu.VMEM((2, 256, 256), BF16),
            pltpu.VMEM((128, 512), BF16),
            pltpu.VMEM((128, 512), BF16),
            pltpu.VMEM((16, 1024), F32),
            pltpu.VMEM((64, 512), BF16),
            block,
            block,
            block,
            block,
            block,
            block,
            block,
            block,
            pltpu.VMEM((2, 128, 512), BF16),
            pltpu.VMEM((2, 128, 512), BF16),
            pltpu.VMEM((2, 256, 256), BF16),
            pltpu.VMEM((2, 256, 256), BF16),
            pltpu.VMEM((NZ, 48, 128), BF16),
            pltpu.VMEM((NZ, 48, 128), BF16),
            pltpu.VMEM((NZ, 208, 128), BF16),
            pltpu.VMEM((7, 208, 128), BF16),
            pltpu.VMEM((8, 208, 128), BF16),
            pltpu.VMEM((NZ, 96, 128), BF16),
            pltpu.VMEM((7, 96, 128), BF16),
            pltpu.VMEM((8, 96, 128), BF16),
            pltpu.VMEM((208, 128), F32),
            pltpu.VMEM((NZ, 144, 128), BF16),
            pltpu.VMEM((NZ, 208, 128), BF16),
            pltpu.VMEM((192, 1024), BF16),
            pltpu.VMEM((2, 192, 1024), BF16),
            pltpu.VMEM((64, 256), BF16),
            pltpu.VMEM((72, 1024), F32),
            dma((2,)),
            *[dma((NE,)) for _ in range(8)],
            dma((NZ,)),
            dma((NZ,)),
            *[dma((n * len(A_SUBS),)) for n in (7, 7, 8, 8)],
            *[dma((n * len(B_SUBS),)) for n in (7, 7, 8, 8)],
            *[dma((n * len(H_SUBS),)) for n in (8, 8, 7, 7)],
            *[dma((n * len(S_SUBS),)) for n in (8, 8, 7, 7)],
        ],
        compiler_params=pltpu.CompilerParams(
            collective_id=0, has_side_effects=True, vmem_limit_bytes=60 * 1024 * 1024
        ),
    )(
        tokens,
        route_ids.T,
        route_weight.T,
        out_cot,
        base_codes[0],
        base_scales.reshape(16, 448),
        adapter_down.reshape(64, 448),
        adapter_up[0],
        magnitude[0],
        down_codes[0].T,
        down_scales[0],
    )
    layer_out, input_grad, grad_down, grad_up, grad_mag = pl.pallas_call(
        emit,
        out_shape=out_shape,
        in_specs=[vmem] * 5,
        out_specs=(vmem,) * 5,
        compiler_params=pltpu.CompilerParams(vmem_limit_bytes=60 * 1024 * 1024),
    )(*outs)
    return (layer_out, input_grad, grad_down[None], grad_up[None], grad_mag[None])


def solution(mesh):
    in_specs = (
        P("expert", "dp"),
        P("expert", None),
        P("expert", None),
        P("expert", "dp"),
        P("expert", None, "dp", None),
        P("expert", None, None, "dp"),
        P("expert", None, None, "dp"),
        P("expert", None, None, None),
        P("expert", None, None),
        P("expert", None, "dp"),
        P("expert", None, "dp"),
    )
    out_specs = (
        P("expert", "dp"),
        P("expert", "dp"),
        P("expert", None, None, "dp"),
        P("expert", None, None, None),
        P("expert", None, None),
    )
    return jax.shard_map(body, mesh=mesh, in_specs=in_specs, out_specs=out_specs, check_vma=False)
```

```python
import jax
import jax.numpy as jnp
from jax import lax
from jax.experimental import pallas as pl
from jax.experimental.pallas import tpu as pltpu
from jax.sharding import PartitionSpec as P

EPSILON = 1e-06
MESH = pl.DeviceIdType.MESH
F32 = jnp.float32
BF16 = jnp.bfloat16
NZ = 16
NE = 64
A_SUBS = ((0, 96), (96, 112))
B_SUBS = ((0, 96),)
H_SUBS = ((0, 144),)
S_SUBS = ((0, 96), (96, 112))


def nn(a, b):
    return jnp.dot(a, b, preferred_element_type=F32)


def nt(a, b):
    return lax.dot_general(a, b, (((1,), (1,)), ((), ())), preferred_element_type=F32)


def iota(shape, dim):
    return lax.broadcasted_iota(jnp.int32, shape, dim)


def split(v):
    hi = v.astype(BF16)
    return hi, (v - hi.astype(F32)).astype(BF16)


def kernel(
    tok_ref,
    ids_ref,
    w_ref,
    cot_ref,
    codes_hbm,
    scales_ref,
    down_ref,
    up_ref,
    mag_ref,
    dcodes_hbm,
    dscales_ref,
    layer_ref,
    igrad_ref,
    gdown_ref,
    gup_ref,
    gmag_ref,
    codes,
    dcodes,
    hi,
    lo,
    dbase,
    xin,
    xcot,
    tpose,
    upad,
    perm,
    gtc,
    gtw,
    colsq,
    dpad,
    send_in,
    recv_in,
    send_cot,
    recv_cot,
    send_out,
    recv_out,
    send_grad,
    recv_grad,
    xs,
    cs,
    yout,
    ygrad,
    eown,
    erecv,
    a_own,
    a_right,
    a_left,
    b_own,
    b_right,
    b_left,
    a_sum,
    ag_h,
    ag_s,
    hid,
    sgu,
    lowt,
    rank,
    wsem,
    in_s,
    in_r,
    cot_s,
    cot_r,
    out_s,
    out_r,
    grad_s,
    grad_r,
    es,
    er,
    a_rs,
    a_rr,
    a_ls,
    a_lr,
    b_rs,
    b_rr,
    b_ls,
    b_lr,
    h_rs,
    h_rr,
    h_ls,
    h_lr,
    s_rs,
    s_rr,
    s_ls,
    s_lr,
):
    me = lax.axis_index("expert")
    z = lax.axis_index("dp")
    mx = lax.div(me, 16)
    my = lax.rem(lax.div(me, 2), 8)
    mc = lax.rem(me, 2)
    right = lax.rem(z + 1, NZ)
    left = lax.rem(z + NZ - 1, NZ)
    mate = me + 1 - 2 * mc

    wcopy = pltpu.make_async_copy(codes_hbm, codes, wsem.at[0])
    dcopy = pltpu.make_async_copy(dcodes_hbm, dcodes, wsem.at[1])
    wcopy.start()
    dcopy.start()

    def chip_of(o):
        px = lax.rem(mx + lax.div(o, 8), 4)
        py = lax.rem(my + lax.rem(o, 8), 8)
        return (px * 8 + py) * 2

    def for_peers(fn, lo_chip=0, hi_chip=32):
        if lo_chip == 0:
            fn(1, mate)

        @pl.loop(max(lo_chip, 1), hi_chip)
        def _(o):
            chip = chip_of(o)
            fn(2 * o, chip + mc)
            fn(2 * o + 1, chip + 1 - mc)

    barrier = pltpu.get_barrier_semaphore()
    for_peers(
        lambda k, peer: pl.semaphore_signal(
            barrier, inc=1, device_id={"expert": peer}, device_id_type=MESH
        )
    )

    @pl.loop(1, NZ)
    def _(k):
        pl.semaphore_signal(
            barrier, inc=1, device_id={"dp": lax.rem(z + k, NZ)}, device_id_type=MESH
        )

    dup = jnp.where((iota((64, 128), 1) & 63) == iota((64, 128), 0), 1.0, 0.0).astype(BF16)
    ids2 = nn(ids_ref[...].astype(F32).astype(BF16), dup)
    w2 = nn(w_ref[...], dup)
    shape = (512, 128)
    row = iota(shape, 0)
    col = iota(shape, 1)
    exp_of = lax.shift_right_logical(row, 3).astype(F32)
    present = jnp.zeros(shape, F32)
    wt = jnp.zeros(shape, F32)
    for k in range(8):
        match = ids2[k : k + 1, :] == exp_of
        present = present + jnp.where(match, 1.0, 0.0)
        wt = wt + jnp.where(match, w2[k : k + 1, :], 0.0)
    ti = iota((128, 128), 0)
    tj = iota((128, 128), 1)
    tri = jnp.where((ti < tj) & ((tj >= 64) == (ti >= 64)), 1.0, 0.0).astype(BF16)
    position = nn(present.astype(BF16), tri)
    slot = (row & 3).astype(F32)
    same_half = (lax.shift_right_logical(row, 2) & 1) == lax.shift_right_logical(col, 6)
    choose = jnp.where((present > 0.5) & (position == slot) & same_half, 1.0, 0.0)
    chosen_w = choose * wt

    def stack(dst, src):
        dst[64:128, 128:256] = jnp.zeros((64, 128), BF16)
        dst[0:64, :] = src[:, 0:256]
        dst[64:128, 0:192] = src[:, 256:448]

    stack(xin, tok_ref)
    stack(xcot, cot_ref)
    send_in[...] = nn(choose.astype(BF16), xin[...]).reshape(NE, 8, 256).astype(BF16)
    send_cot[...] = nn(chosen_w.astype(BF16), xcot[...]).reshape(NE, 8, 256).astype(BF16)

    pl.semaphore_wait(barrier, NE - 1 + NZ - 1)

    class Exchange:
        def __init__(self, src, dst, ssem, rsem):
            self.src, self.dst, self.ssem, self.rsem = src, dst, ssem, rsem

        def copy(self, k, slot, peer):
            return pltpu.make_async_remote_copy(
                src_ref=self.src.at[peer],
                dst_ref=self.dst.at[slot],
                send_sem=self.ssem.at[k],
                recv_sem=self.rsem.at[slot],
                device_id={"expert": peer},
                device_id_type=MESH,
            )

        def start(self, lo_chip=0, hi_chip=32):
            for_peers(lambda k, peer: self.copy(k, me, peer).start(), lo_chip, hi_chip)

        def keep(self):
            self.dst[me] = self.src[me]

        def wait(self):
            for_peers(lambda k, peer: self.copy(k, peer, peer).wait_recv())

        def drain(self):
            for_peers(lambda k, peer: self.copy(k, me, peer).wait_send())

    x_in = Exchange(send_in, recv_in, in_s, in_r)
    x_cot = Exchange(send_cot, recv_cot, cot_s, cot_r)
    x_out = Exchange(send_out, recv_out, out_s, out_r)
    x_grad = Exchange(send_grad, recv_grad, grad_s, grad_r)
    x_in.start()
    x_cot.start()
    x_in.keep()
    x_cot.keep()

    tpose[88:128, :] = jnp.zeros((40, 512), F32)
    tpose[0:88, 384:512] = jnp.zeros((88, 128), F32)
    tpose[0:16, 0:448] = scales_ref[...]
    tpose[16:80, 0:448] = down_ref[...].astype(F32)
    tpose[80:88, 0:448] = dscales_ref[...]
    dpad[:, 384:512] = jnp.zeros((64, 128), BF16)
    dpad[:, 0:448] = down_ref[...]
    turned = tpose[...].T
    for i in range(4):
        tpose[:, i * 128 : (i + 1) * 128] = turned[i * 128 : (i + 1) * 128, :]
    upad[...] = jnp.zeros((2, 128, 1024), BF16)
    upad[0, 16:48, :] = up_ref[0]
    upad[1, 48:80, :] = up_ref[1]
    hi[:, 448:512, :] = jnp.zeros((2, 64, 1024), BF16)
    lo[:, 448:512, :] = jnp.zeros((2, 64, 1024), BF16)
    dbase[448:512, :] = jnp.zeros((64, 1024), BF16)
    colsq[...] = jnp.zeros((16, 1024), F32)
    wcopy.wait()

    def turned_rows(blk):
        d0 = blk * 64
        return tpose[d0 % 128 : d0 % 128 + 64, (d0 // 128) * 128 : (d0 // 128) * 128 + 128]

    for blk in range(7):
        d0 = blk * 64
        turn = turned_rows(blk)
        turn_b = turn.astype(BF16)
        for i in range(2):
            for fb in range(8):
                f0 = fb * 128
                scale = turn[:, i * 8 + fb : i * 8 + fb + 1]
                val = codes[i, d0 : d0 + 64, f0 : f0 + 128].astype(F32) * scale
                val = val + nn(turn_b, upad[i, :, f0 : f0 + 128])
                top, bottom = split(val)
                hi[i, d0 : d0 + 64, f0 : f0 + 128] = top
                lo[i, d0 : d0 + 64, f0 : f0 + 128] = bottom
                sq = (val * val).reshape(8, 8, 128).sum(axis=0)
                colsq[i * 8 : i * 8 + 8, f0 : f0 + 128] = colsq[i * 8 : i * 8 + 8, f0 : f0 + 128] + sq

    for q in range(8):
        f0 = q * 128
        c0 = jnp.sum(colsq[0:8, f0 : f0 + 128], axis=0, keepdims=True)
        c1 = jnp.sum(colsq[8:16, f0 : f0 + 128], axis=0, keepdims=True)
        rows = iota((16, 128), 0)
        cblock = jnp.where(rows == 0, c0, jnp.where(rows == 1, c1, 0.0)).astype(BF16)
        for h in range(2):
            dn = dpad[h * 32 : (h + 1) * 32, :]
            proj = nn(dn, hi[h, :, f0 : f0 + 128]) + nn(dn, lo[h, :, f0 : f0 + 128])
            eown[2 * q + h, 0:32, :] = proj.astype(BF16)
            eown[2 * q + h, 32:48, :] = cblock

    def early(k, slot, peer):
        return pltpu.make_async_remote_copy(
            src_ref=eown.at[peer],
            dst_ref=erecv.at[slot],
            send_sem=es.at[k],
            recv_sem=er.at[slot],
            device_id={"dp": peer},
            device_id_type=MESH,
        )

    @pl.loop(1, NZ)
    def _(k):
        early(k, z, lax.rem(z + k, NZ)).start()

    pr = iota((256, 256), 0)
    pc = iota((256, 256), 1)

    def target(v):
        return (
            8 * (v & 31)
            + (lax.shift_right_logical(v, 5) & 3)
            + 4 * lax.shift_right_logical(v, 7)
        )

    perm[0] = jnp.where(pc == target(pr), 1.0, 0.0).astype(BF16)
    perm[1] = jnp.where(pr == target(pc), 1.0, 0.0).astype(BF16)
    for p in range(8, NZ):
        a_own[p, 192:208, :] = jnp.zeros((16, 128), BF16)
    yout[...] = jnp.zeros((2, 256, 256), BF16)
    ygrad[...] = jnp.zeros((2, 256, 256), BF16)

    dcopy.wait()
    for blk in range(7):
        d0 = blk * 64
        turn = turned_rows(blk)
        for fb in range(8):
            f0 = fb * 128
            dbase[d0 : d0 + 64, f0 : f0 + 128] = (
                dcodes[d0 : d0 + 64, f0 : f0 + 128].astype(F32) * turn[:, 80 + fb : 81 + fb]
            ).astype(BF16)
    gtc[...] = choose.T.astype(BF16)
    gtw[...] = chosen_w.T.astype(BF16)

    def arrange(recv, dst):
        for h in range(2):
            block = recv[h * 32 : (h + 1) * 32].astype(F32).reshape(256, 256).astype(BF16)
            got = nn(perm[0], block).astype(BF16)
            dst[h, :, 0:256] = got[0:128]
            dst[h, :, 256:512] = got[128:256]

    def lanes_of(c):
        return pl.ds(pl.multiple_of(lax.div(c, 2) * 128, 128), 128)

    def chunk_a(c):
        h = lax.rem(c, 2)
        rows = xs[h, 0:96, :]
        a_own[c, 0:96, :] = nn(rows, hi[0, :, lanes_of(c)]).astype(BF16)
        a_own[c, 96:192, :] = nn(rows, hi[1, :, lanes_of(c)]).astype(BF16)

    def chunk_b(c):
        h = lax.rem(c, 2)
        b_own[c] = nn(cs[h, 0:96, :], dbase[:, lanes_of(c)]).astype(BF16)

    def hop(src, dst, ssem, rsem, to):
        return pltpu.make_async_remote_copy(
            src_ref=src,
            dst_ref=dst,
            send_sem=ssem,
            recv_sem=rsem,
            device_id={"dp": to},
            device_id_type=MESH,
        )

    class Reduce:
        def __init__(self, own, bufs, sems, subs, make):
            self.own, self.bufs, self.sems, self.subs, self.make = own, bufs, sems, subs, make

        def chunk(self, t, d):
            return lax.rem(z + 7 - t, NZ) if d == 0 else lax.rem(z + 8 + t, NZ)

        def copy(self, t, sub, d, first):
            r0, n = self.subs[sub]
            buf, (ssem, rsem) = self.bufs[d], self.sems[d]
            rows = pl.ds(r0, n)
            src = self.own.at[self.chunk(t, d), rows, :] if first else buf.at[t - 1, rows, :]
            at = t * len(self.subs) + sub
            return hop(src, buf.at[t, rows, :], ssem.at[at], rsem.at[at], (right, left)[d])

        def begin(self):
            for d in (0, 1):
                self.make(self.chunk(0, d))
                for sub in range(len(self.subs)):
                    self.copy(0, sub, d, True).start()

        def step(self, t, dirs=(0, 1)):
            for d in dirs:
                self.make(self.chunk(t, d))
            for sub in range(len(self.subs)):
                r0, n = self.subs[sub]
                rows = pl.ds(r0, n)
                for d in dirs:
                    buf = self.bufs[d]
                    self.copy(t - 1, sub, d, True).wait_recv()
                    buf[t - 1, rows, :] = (
                        buf[t - 1, rows, :].astype(F32)
                        + self.own[self.chunk(t, d), rows, :].astype(F32)
                    ).astype(BF16)
                    self.copy(t, sub, d, False).start()

        def total(self):
            for sub in range(len(self.subs)):
                self.copy(6, sub, 0, True).wait_recv()
                self.copy(7, sub, 1, True).wait_recv()
            return (
                self.own[z].astype(F32) + self.bufs[0][6].astype(F32) + self.bufs[1][7].astype(F32)
            )

        def drain(self):
            @pl.loop(0, 7)
            def _(t):
                for sub in range(len(self.subs)):
                    self.copy(t, sub, 0, True).wait_send()
                    self.copy(t, sub, 1, True).wait_send()

            for sub in range(len(self.subs)):
                self.copy(7, sub, 1, True).wait_send()

    class Gather:
        def __init__(self, buf, sems, subs):
            self.buf, self.sems, self.subs = buf, sems, subs

        def copy(self, t, sub, d, chunk):
            r0, n = self.subs[sub]
            ssem, rsem = self.sems[d]
            ref = self.buf.at[chunk, pl.ds(r0, n), :]
            at = t * len(self.subs) + sub
            return hop(ref, ref, ssem.at[at], rsem.at[at], (right, left)[d])

        def sent(self, t, sub, d):
            return self.copy(t, sub, d, lax.rem(z + NZ - t, NZ) if d == 0 else lax.rem(z + t, NZ))

        def come(self, t, sub, d):
            return self.copy(
                t, sub, d, lax.rem(z + NZ - 1 - t, NZ) if d == 0 else lax.rem(z + 1 + t, NZ)
            )

        def begin(self):
            for sub in range(len(self.subs)):
                for d in (0, 1):
                    self.sent(0, sub, d).start()

        def step(self, t, dirs=(0, 1)):
            for sub in range(len(self.subs)):
                for d in dirs:
                    self.come(t - 1, sub, d).wait_recv()
                    self.sent(t, sub, d).start()

        def finish(self):
            for sub in range(len(self.subs)):
                self.come(6, sub, 1).wait_recv()
            for sub in range(len(self.subs)):
                self.come(7, sub, 0).wait_recv()

        def drain(self):
            @pl.loop(0, 7)
            def _(t):
                for sub in range(len(self.subs)):
                    self.sent(t, sub, 0).wait_send()
                    self.sent(t, sub, 1).wait_send()

            for sub in range(len(self.subs)):
                self.sent(7, sub, 0).wait_send()

    red_a = Reduce(a_own, (a_right, a_left), ((a_rs, a_rr), (a_ls, a_lr)), A_SUBS, chunk_a)
    red_b = Reduce(b_own, (b_right, b_left), ((b_rs, b_rr), (b_ls, b_lr)), B_SUBS, chunk_b)
    gat_h = Gather(ag_h, ((h_rs, h_rr), (h_ls, h_lr)), H_SUBS)
    gat_s = Gather(ag_s, ((s_rs, s_rr), (s_ls, s_lr)), S_SUBS)

    x_in.wait()
    arrange(recv_in, xs)
    low = nt(dpad[...], xs[...].reshape(256, 512)).astype(BF16)
    for p in range(8):
        a_own[p, 192:208, :] = low[
            (p // 2) * 16 : (p // 2) * 16 + 16, (p % 2) * 128 : (p % 2) * 128 + 128
        ]
    red_a.begin()

    @pl.loop(1, 4)
    def _(t):
        red_a.step(t)

    x_cot.wait()
    arrange(recv_cot, cs)
    red_b.begin()

    @pl.loop(4, 7)
    def _(t):
        red_a.step(t)
        red_b.step(t - 3)

    red_a.step(7, (1,))
    chunk_a(z)
    red_b.step(4)
    chunk_b(z)

    @pl.loop(1, NZ)
    def _(k):
        peer = lax.rem(z + k, NZ)
        early(k, peer, peer).wait_recv()

    erecv[z] = eown[z]
    esum = erecv[0].astype(F32)
    for p in range(1, NZ):
        esum = esum + erecv[p].astype(F32)
    mag = mag_ref[:, lanes_of(z)]
    norm = jnp.sqrt(esum[32:34, :] + EPSILON)
    ratio = mag / norm

    total = red_a.total()
    a_sum[...] = total
    gate_val = total[0:96] * ratio[0:1]
    up_val = total[96:192] * ratio[1:2]
    ag_h[z, 0:96, :] = (gate_val * jax.nn.sigmoid(gate_val) * up_val).astype(BF16)
    ag_h[z, 96:112, :] = total[192:208].astype(BF16)
    ag_h[z, 112:144, :] = esum[0:32, :].astype(BF16)
    gat_h.begin()

    @pl.loop(5, 7)
    def _(t):
        red_b.step(t)
        gat_h.step(t - 4)

    red_b.step(7, (1,))
    gat_h.step(3)

    unit = red_b.total()
    gate_pre, up_pre = a_sum[0:96, :], a_sum[96:192, :]
    gate_val = gate_pre * ratio[0:1]
    up_val = up_pre * ratio[1:2]
    sig = jax.nn.sigmoid(gate_val)
    gate_grad = unit * up_val * sig * (1.0 + gate_val * (1.0 - sig))
    up_grad = unit * (gate_val * sig)
    gm0 = jnp.sum(gate_grad * gate_pre, axis=0, keepdims=True) / norm[0:1]
    gm1 = jnp.sum(up_grad * up_pre, axis=0, keepdims=True) / norm[1:2]
    sh0 = mag[0:1] * gm0 / (norm[0:1] * norm[0:1])
    sh1 = mag[1:2] * gm1 / (norm[1:2] * norm[1:2])
    rows = iota((16, 128), 0)
    extra = jnp.where(
        rows == 0, gm0, jnp.where(rows == 1, gm1, jnp.where(rows == 2, sh0, jnp.where(rows == 3, sh1, 0.0)))
    )
    ag_s[z, 0:96, :] = (gate_grad * ratio[0:1]).astype(BF16)
    ag_s[z, 96:192, :] = (up_grad * ratio[1:2]).astype(BF16)
    ag_s[z, 192:208, :] = extra.astype(BF16)
    gat_s.begin()

    @pl.loop(4, 7)
    def _(t):
        gat_h.step(t)
        gat_s.step(t - 3)

    gat_h.step(7, (0,))
    gat_s.step(4)
    gat_h.finish()

    def give_back(value, y, send):
        for h in range(2):
            r = slice(h * 96, (h + 1) * 96)
            y[h, 0:96, :] = value[r, 0:256]
            y[h, 128:224, :] = value[r, 256:512]
            send[h * 32 : (h + 1) * 32] = nn(perm[1], y[h]).reshape(32, 8, 256).astype(BF16)

    for q in range(8):
        f0 = q * 128
        for h in range(2):
            hid[h * 96 : (h + 1) * 96, f0 : f0 + 128] = ag_h[2 * q + h, 0:96, :]
    give_back(nt(hid[...], dbase[...]).astype(BF16), yout, send_out)
    gat_s.step(5)
    x_out.start(0, 16)
    gat_s.step(6)
    x_out.start(16, 32)
    gat_s.step(7, (0,))
    x_out.keep()
    gat_s.finish()

    for q in range(8):
        f0 = q * 128
        for h in range(2):
            sgu[0, h * 96 : (h + 1) * 96, f0 : f0 + 128] = ag_s[2 * q + h, 0:96, :]
            sgu[1, h * 96 : (h + 1) * 96, f0 : f0 + 128] = ag_s[2 * q + h, 96:192, :]
    give_back((nt(sgu[0], hi[0]) + nt(sgu[1], hi[1])).astype(BF16), ygrad, send_grad)
    x_grad.start()
    x_grad.keep()

    for q in range(8):
        f0 = q * 128
        both = ag_s[2 * q, 192:208, :].astype(F32) + ag_s[2 * q + 1, 192:208, :].astype(F32)
        gmag_ref[:, f0 : f0 + 128] = both[0:2]
        rank[64:72, f0 : f0 + 128] = both[0:8]
        rank[0:32, f0 : f0 + 128] = ag_h[2 * q, 112:144, :].astype(F32)
        rank[32:64, f0 : f0 + 128] = ag_h[2 * q + 1, 112:144, :].astype(F32)
    for p in range(8):
        lowt[(p // 2) * 16 : (p // 2) * 16 + 16, (p % 2) * 128 : (p % 2) * 128 + 128] = ag_h[p, 96:112, :]
    for i in range(2):
        shrink = rank[66 + i : 67 + i, :]
        back_t = nt(up_ref[i], sgu[i]).astype(BF16)
        down_t = nn(back_t[:, 0:96], xs[0, 0:96, :]) + nn(back_t[:, 96:192], xs[1, 0:96, :])
        uh, ul = split(up_ref[i].astype(F32) * shrink)
        down_t = down_t - (nt(uh, hi[i]) + nt(uh, lo[i]) + nt(ul, hi[i]))
        gdown_ref[i] = down_t[:, 0:448]
        rows_i = slice(i * 32, (i + 1) * 32)
        grow = nn(lowt[rows_i, 0:96], sgu[i, 0:96, :]) + nn(lowt[rows_i, 128:224], sgu[i, 96:192, :])
        gup_ref[i] = grow - rank[rows_i, :] * shrink

    x_in.drain()
    x_cot.drain()
    red_a.drain()
    red_b.drain()
    gat_h.drain()
    gat_s.drain()

    @pl.loop(1, NZ)
    def _(k):
        early(k, z, lax.rem(z + k, NZ)).wait_send()

    def combine(exchange, mat, recv, out):
        exchange.wait()
        got = nn(mat[...], recv[...].astype(F32).reshape(512, 256).astype(BF16)).astype(BF16)
        out[:, 0:256] = got[0:64]
        out[:, 256:448] = got[64:128, 0:192]

    combine(x_out, gtw, recv_out, layer_ref)
    combine(x_grad, gtc, recv_grad, igrad_ref)
    x_out.drain()
    x_grad.drain()


def emit(*refs):
    for src, dst in zip(refs[:5], refs[5:]):
        dst[...] = src[...]


def body(tokens, route_ids, route_weight, out_cot, base_codes, base_scales, adapter_down, adapter_up, magnitude, down_codes, down_scales):
    vmem = pl.BlockSpec(memory_space=pltpu.VMEM)
    hbm = pl.BlockSpec(memory_space=pl.ANY)
    dma = pltpu.SemaphoreType.DMA
    block = pltpu.VMEM((NE, 8, 256), BF16)
    out_shape = (
        jax.ShapeDtypeStruct((64, 448), BF16),
        jax.ShapeDtypeStruct((64, 448), BF16),
        jax.ShapeDtypeStruct((2, 32, 448), F32),
        jax.ShapeDtypeStruct((2, 32, 1024), F32),
        jax.ShapeDtypeStruct((2, 1024), F32),
    )
    outs = pl.pallas_call(
        kernel,
        out_shape=out_shape,
        in_specs=[vmem, vmem, vmem, vmem, hbm, vmem, vmem, vmem, vmem, hbm, vmem],
        out_specs=(vmem,) * 5,
        scratch_shapes=[
            pltpu.VMEM((2, 448, 1024), BF16),
            pltpu.VMEM((448, 1024), BF16),
            pltpu.VMEM((2, 512, 1024), BF16),
            pltpu.VMEM((2, 512, 1024), BF16),
            pltpu.VMEM((512, 1024), BF16),
            pltpu.VMEM((128, 256), BF16),
            pltpu.VMEM((128, 256), BF16),
            pltpu.VMEM((128, 512), F32),
            pltpu.VMEM((2, 128, 1024), BF16),
            pltpu.VMEM((2, 256, 256), BF16),
            pltpu.VMEM((128, 512), BF16),
            pltpu.VMEM((128, 512), BF16),
            pltpu.VMEM((16, 1024), F32),
            pltpu.VMEM((64, 512), BF16),
            block,
            block,
            block,
            block,
            block,
            block,
            block,
            block,
            pltpu.VMEM((2, 128, 512), BF16),
            pltpu.VMEM((2, 128, 512), BF16),
            pltpu.VMEM((2, 256, 256), BF16),
            pltpu.VMEM((2, 256, 256), BF16),
            pltpu.VMEM((NZ, 48, 128), BF16),
            pltpu.VMEM((NZ, 48, 128), BF16),
            pltpu.VMEM((NZ, 208, 128), BF16),
            pltpu.VMEM((7, 208, 128), BF16),
            pltpu.VMEM((8, 208, 128), BF16),
            pltpu.VMEM((NZ, 96, 128), BF16),
            pltpu.VMEM((7, 96, 128), BF16),
            pltpu.VMEM((8, 96, 128), BF16),
            pltpu.VMEM((208, 128), F32),
            pltpu.VMEM((NZ, 144, 128), BF16),
            pltpu.VMEM((NZ, 208, 128), BF16),
            pltpu.VMEM((192, 1024), BF16),
            pltpu.VMEM((2, 192, 1024), BF16),
            pltpu.VMEM((64, 256), BF16),
            pltpu.VMEM((72, 1024), F32),
            dma((2,)),
            *[dma((NE,)) for _ in range(8)],
            dma((NZ,)),
            dma((NZ,)),
            *[dma((n * len(A_SUBS),)) for n in (7, 7, 8, 8)],
            *[dma((n * len(B_SUBS),)) for n in (7, 7, 8, 8)],
            *[dma((n * len(H_SUBS),)) for n in (8, 8, 7, 7)],
            *[dma((n * len(S_SUBS),)) for n in (8, 8, 7, 7)],
        ],
        compiler_params=pltpu.CompilerParams(
            collective_id=0, has_side_effects=True, vmem_limit_bytes=60 * 1024 * 1024
        ),
    )(
        tokens,
        route_ids.T,
        route_weight.T,
        out_cot,
        base_codes[0],
        base_scales.reshape(16, 448),
        adapter_down.reshape(64, 448),
        adapter_up[0],
        magnitude[0],
        down_codes[0].T,
        down_scales[0],
    )
    layer_out, input_grad, grad_down, grad_up, grad_mag = pl.pallas_call(
        emit,
        out_shape=out_shape,
        in_specs=[vmem] * 5,
        out_specs=(vmem,) * 5,
        compiler_params=pltpu.CompilerParams(vmem_limit_bytes=60 * 1024 * 1024),
    )(*outs)
    return (layer_out, input_grad, grad_down[None], grad_up[None], grad_mag[None])


def solution(mesh):
    in_specs = (
        P("expert", "dp"),
        P("expert", None),
        P("expert", None),
        P("expert", "dp"),
        P("expert", None, "dp", None),
        P("expert", None, None, "dp"),
        P("expert", None, None, "dp"),
        P("expert", None, None, None),
        P("expert", None, None),
        P("expert", None, "dp"),
        P("expert", None, "dp"),
    )
    out_specs = (
        P("expert", "dp"),
        P("expert", "dp"),
        P("expert", None, None, "dp"),
        P("expert", None, None, None),
        P("expert", None, None),
    )
    return jax.shard_map(body, mesh=mesh, in_specs=in_specs, out_specs=out_specs, check_vma=False)
```
